512 devices in a mesh: seq: 64 (over x, y, core), chan: 8 (over z).
Axes of the slice: x: 4, y: 8, z: 8, core: 2. Of those that a mesh axis runs over, the one named last changes fastest.
Arguments:
- gate_outer: bfloat16 [8192, 4096], P('seq', 'chan'), may hold values from -520 to 520
- gate_inner: bfloat16 [8192, 4096], P('seq', 'chan'), may hold values from -6 to 6
- value_in: bfloat16 [8192, 4096], P('seq', 'chan'), may hold values from -6 to 6
- pole_rates: float32 [8, 4096], P(None, 'chan'), may hold values from 0 to 1, as said below
- pole_weights: float32 [8, 4096], P(None, 'chan'), may hold values from -4 to 4
- skip_gain: float32 [4096], P('chan'), may hold values from -1 to 1
- query_rows: bfloat16 [8192, 4096], P('seq', 'chan'), may hold values from -6 to 6
- key_rows: bfloat16 [8192, 4096], P('seq', 'chan'), may hold values from -6 to 6
Outputs:
- mixed: bfloat16 [8192, 4096], P('seq', 'chan')
The draws below stay inside these ranges and needn't reach their ends.
Inputs may be any that keep to these rules, and one draw needn't show every extreme that they name: `pole_rates`: each rate is positive and at most 1/30.
All inputs are finite; a program needn't handle non-finite values.
Results may differ from the reference program's by a relative error of at most 0.0065.
Values may be sent and summed in bfloat16 or wider, within the bound.
A program may use at most 128 MiB of HBM per device.

```python
import math
import jax
import jax.numpy as jnp
from jax import lax

HEADS = 32
HD = 128
POLES = 8
CH = 4096
LENGTH = 8192


def draw_query_rows(key, part):
    base_key = jax.random.fold_in(key, 11)
    rows_drawn = jnp.clip(jax.random.normal(base_key, (LENGTH, CH), jnp.float32), -6.0, 6.0)
    return rows_drawn.astype(jnp.bfloat16)


def draw_key_rows(key, part):
    base_key = jax.random.fold_in(key, 12)
    rows_drawn = jnp.clip(jax.random.normal(base_key, (LENGTH, CH), jnp.float32), -6.0, 6.0)
    return rows_drawn.astype(jnp.bfloat16)


def draw_gate_outer(key, part):
    parts_key = jax.random.split(jax.random.fold_in(key, 21), 3)
    column = jnp.arange(CH, dtype=jnp.float32) / CH
    col_scale = jnp.exp(jax.random.uniform(parts_key[1], (1, CH), jnp.float32, 0.0, math.log(10.0)))
    col_scale = col_scale * jnp.exp(0.5 * math.log(3.0) * column)[None, :]
    row_scale = jnp.exp(jax.random.uniform(parts_key[0], (LENGTH, 1), jnp.float32, 0.0, math.log(10.0)))
    noise = jnp.clip(jax.random.normal(parts_key[2], (LENGTH, CH), jnp.float32), -3.0, 3.0)
    corner = 3.0 * 10.0 * 10.0 * math.sqrt(3.0)
    drawn = noise * row_scale * col_scale
    drawn = drawn.at[LENGTH - 1, CH - 1].set(corner)
    return drawn.astype(jnp.bfloat16)


def draw_pole_rates(key, part):
    parts_key = jax.random.split(jax.random.fold_in(key, 31), 3)
    slow = jnp.exp(jax.random.uniform(parts_key[0], (POLES, CH), jnp.float32, math.log(0.2 / LENGTH), math.log(2.0 / LENGTH)))
    fast = jnp.exp(jax.random.uniform(parts_key[1], (POLES, CH), jnp.float32, math.log(1.0 / 50.0), math.log(1.0 / 30.0)))
    share = 0.5
    picked = jax.random.bernoulli(parts_key[2], share, (POLES, CH))
    return jnp.where(picked, slow, fast).astype(jnp.float32)


def shard_levels(own_key, dims, pieces, least, high):
    gain, own = 1.0, jax.random.fold_in(own_key, 6)
    for position, shards_of in pieces:
        heights = jnp.exp(jax.random.uniform(jax.random.fold_in(own, position), (shards_of,), jnp.float32, least / len(pieces), high / len(pieces)))
        gain = gain * jnp.repeat(heights, dims[position] // shards_of).reshape([-1 if axis == position else 1 for axis in range(len(dims))])
    return gain


def gaussian(rng, extent, deviation, bound, pieces=(), kind=jnp.bfloat16):
    loudness = shard_levels(rng, extent, pieces, -0.22, 0.18) if pieces else 1.0
    entries = jax.random.normal(rng, extent, jnp.float32) * deviation * loudness
    return jnp.minimum(jnp.maximum(entries, -bound), bound).astype(kind)


def setup_inputs(seed: int = 0) -> dict:
    seeds = jax.random.split(jax.random.key(seed), 9)
    gate_outer = draw_gate_outer(jax.random.fold_in(seeds[8], 71), 0)
    gate_inner = gaussian(seeds[1], (LENGTH, CH), 1.0, 6.0, ((0, 64), (1, 8)))
    value_in = gaussian(seeds[2], (LENGTH, CH), 1.0, 6.0, ((0, 64), (1, 8)))
    pole_rates = draw_pole_rates(jax.random.fold_in(seeds[8], 71), 0)
    pole_weights = gaussian(seeds[4], (POLES, CH), 1.0, 4.0, ((1, 8),), jnp.float32)
    skip_gain = jnp.clip(jax.random.uniform(seeds[5], (CH,), jnp.float32, -1.0, 1.0) * shard_levels(seeds[5], (CH,), ((0, 8),), -0.4, 0.0), -1.0, 1.0)
    query_rows = draw_query_rows(jax.random.fold_in(seeds[8], 71), 0)
    key_rows = draw_key_rows(jax.random.fold_in(seeds[8], 71), 0)
    return dict(gate_outer=gate_outer, gate_inner=gate_inner, value_in=value_in, pole_rates=pole_rates, pole_weights=pole_weights, skip_gain=skip_gain, query_rows=query_rows, key_rows=key_rows)


def convolve(gated, pole_rates, pole_weights):
    decay = jnp.exp(-pole_rates)
    weighting = pole_weights * jnp.sqrt(pole_rates)

    def advance(modal_state, column):
        modal_state = decay * modal_state + column[None, :]
        return (modal_state, lax.optimization_barrier(jnp.sum(weighting * modal_state, axis=0)))
    start_state = jnp.zeros(pole_rates.shape, jnp.float32)
    final_state, filtered = lax.scan(advance, start_state, gated)
    return filtered

def attend_head(query_head, key_head, value_head):
    total = query_head.shape[0]
    block_rows = min(512, total)
    key_pos = jnp.arange(total, dtype=jnp.int32)
    score_scale = HD ** (-0.5)

    def one_block(block_index):
        first_row = (block_index * block_rows).astype(jnp.int32)
        rows_here = lax.dynamic_slice_in_dim(query_head, first_row, block_rows, 0)
        scores = jnp.dot(rows_here, key_head.T, preferred_element_type=jnp.float32) * score_scale
        query_pos = first_row + jnp.arange(block_rows, dtype=jnp.int32)
        visible = key_pos[None, :] <= query_pos[:, None]
        scores = jnp.where(visible, scores, -1e+30)
        top_score = lax.optimization_barrier(jnp.max(scores, axis=1, keepdims=True))
        expo = jnp.where(visible, jnp.exp(scores - top_score), 0.0)
        totals = lax.optimization_barrier(jnp.sum(expo, axis=1, keepdims=True))
        summed = jnp.dot(expo.astype(jnp.bfloat16), value_head, preferred_element_type=jnp.float32)
        return (summed / totals).astype(jnp.bfloat16)
    blocks = lax.map(one_block, jnp.arange(total // block_rows, dtype=jnp.int32))
    return blocks.reshape(total, value_head.shape[1])

def reference(gate_outer, gate_inner, value_in, pole_rates, pole_weights, skip_gain, query_rows, key_rows):
    gated = gate_inner.astype(jnp.float32) * value_in.astype(jnp.float32)
    filtered = convolve(gated, pole_rates, pole_weights)
    conv_out = gate_outer.astype(jnp.float32) * (filtered + skip_gain[None, :] * gated)
    mean_square = lax.optimization_barrier(jnp.mean(conv_out * conv_out, axis=1, keepdims=True))
    values = (conv_out * lax.rsqrt(mean_square + 1e-06)).astype(jnp.bfloat16)
    total = query_rows.shape[0]

    def per_head(head_index):
        first_col = (head_index * HD).astype(jnp.int32)
        query_head = lax.dynamic_slice_in_dim(query_rows, first_col, HD, 1)
        key_head = lax.dynamic_slice_in_dim(key_rows, first_col, HD, 1)
        value_head = lax.dynamic_slice_in_dim(values, first_col, HD, 1)
        return attend_head(query_head, key_head, value_head)
    outputs = lax.map(per_head, jnp.arange(HEADS, dtype=jnp.int32))
    return jnp.transpose(outputs, (1, 0, 2)).reshape(total, HEADS * HD)
```

```python
import functools
import math

import jax
import jax.numpy as jnp
from jax import lax
from jax.experimental import pallas as pl
from jax.experimental.pallas import tpu as pltpu
from jax.sharding import PartitionSpec as P

HD = 128
CORES = 2
SUB = 32
MESH = pl.DeviceIdType.MESH
NEG = -1e30


def kernel(
    X,
    Y,
    Z,
    go_hbm,
    gi_hbm,
    vi_hbm,
    pr_ref,
    pw_ref,
    sg_ref,
    q_hbm,
    k_hbm,
    o_ref,
    go,
    gi,
    vi,
    g,
    y0,
    cv,
    ct,
    dd,
    fp,
    e_own,
    e_sib,
    tb,
    rb,
    sq,
    vs,
    qb,
    kb,
    vb,
    pt,
    ms,
    ls,
    ac,
    orx,
    fs,
    s_in,
    s_e,
    s_t,
    s_r,
    s_s,
    s_q,
    s_kx,
    s_k,
    s_vx,
    s_v,
    s_m,
    s_o,
):
    T = go.shape[0]
    W = go.shape[1]
    D = Y // 2
    SPAN = float(CORES * T)
    s = lax.axis_index("seq")
    z = lax.axis_index("chan")
    c = lax.rem(s, CORES)
    chip = s // CORES
    y = lax.rem(chip, Y)
    x = chip // Y

    def seq_id(xx, yy, cc):
        return {"seq": (xx * Y + yy) * CORES + cc}

    sib = {"seq": s + 1 - 2 * c}
    peers = [sib]
    peers += [seq_id(x, lax.rem(y + k, Y), c) for k in range(1, Y)]
    peers += [seq_id(lax.rem(x + o, X), y, c) for o in range(1, X)]
    peers += [{"chan": lax.rem(z + k, Z)} for k in range(1, Z)]

    barrier = pltpu.get_barrier_semaphore()
    for p in peers:
        pl.semaphore_signal(barrier, inc=1, device_id=p, device_id_type=MESH)

    cols = lambda h: pl.ds(pl.multiple_of(h * HD, HD), HD)
    in_gi = pltpu.make_async_copy(gi_hbm, gi, s_in.at[0])
    in_vi = pltpu.make_async_copy(vi_hbm, vi, s_in.at[1])
    in_go = pltpu.make_async_copy(go_hbm, go, s_in.at[2])
    in_q = pltpu.make_async_copy(q_hbm.at[:, cols(x)], qb.at[c, x], s_in.at[3])
    in_k = pltpu.make_async_copy(k_hbm.at[:, cols(x)], kb.at[0, x], s_in.at[4])
    in_gi.start()
    in_vi.start()
    in_go.start()
    in_q.start()
    in_k.start()

    def remote(src, dst, sems, n, i, dev):
        return pltpu.make_async_remote_copy(
            src_ref=src,
            dst_ref=dst,
            send_sem=sems.at[i],
            recv_sem=sems.at[n + i],
            device_id=dev,
            device_id_type=MESH,
        )

    rates = pr_ref[...]
    decay = jnp.exp(-rates)
    d_sub = jnp.exp(-float(SUB) * rates)
    wgt = pw_ref[...] * jnp.sqrt(rates)
    chains = T // SUB
    state0 = jnp.zeros(rates.shape, jnp.float32)

    in_gi.wait()
    in_vi.wait()
    g[...] = gi[...].astype(jnp.float32) * vi[...].astype(jnp.float32)

    def scan(emit):
        def body(i, states):
            out = []
            for n in range(chains):
                row = n * SUB + i
                st = decay * states[n] + g[pl.ds(row, 1), :]
                if emit:
                    y0[pl.ds(row, 1), :] = jnp.sum(wgt * st, axis=0, keepdims=True)
                out.append(st)
            return tuple(out)

        return lax.fori_loop(0, SUB, body, (state0,) * chains, unroll=8)

    ends = scan(False)
    total = ends[0]
    for n in range(1, chains):
        total = ends[n] + d_sub * total
    e_own[...] = total

    pl.semaphore_wait(barrier, len(peers))

    e_cp = remote(e_own, e_sib, s_e, 1, 0, sib)
    e_cp.start()

    def x_copy(src, dst, sems, o):
        h = lax.rem(x + o, X)
        return remote(src(h), dst, sems, X, o, seq_id(h, y, c))

    q_cp = [
        x_copy(lambda h: q_hbm.at[:, cols(h)], qb.at[c, x], s_q, o) if o else in_q for o in range(X)
    ]
    k_cp = [
        x_copy(lambda h: k_hbm.at[:, cols(h)], kb.at[0, x], s_kx, o) if o else in_k
        for o in range(X)
    ]
    for o in range(1, X):
        k_cp[o].start()
    for o in range(1, X):
        q_cp[o].start()

    for n in range(Y):
        fp[n] = jnp.exp((-SPAN * n) * rates)
    f_one = jnp.exp(-float(T) * rates)

    e_cp.wait_recv()
    mine, other = e_own[...], e_sib[...]
    first = jnp.where(c == 0, mine, other)
    second = jnp.where(c == 0, other, mine)
    tb[0] = second + f_one * first
    t_cp = [
        remote(tb.at[0], tb.at[k], s_t, Y, k, seq_id(x, lax.rem(y + k, Y), c)) for k in range(1, Y)
    ]
    for k in sorted(range(1, Y), key=lambda k: -min(k, Y - k)):
        t_cp[k - 1].start()

    right = seq_id(x, lax.rem(y + 1, Y), c)
    left = seq_id(x, lax.rem(y + Y - 1, Y), c)

    def offset(i):
        return jnp.where(i < 2, i, X + 1 - i) if X > 2 else i

    def ring(buf, sems, way, d, i):
        piece = lax.rem(x + X - offset(i), X)
        src = d - 1 if way == 0 else (Y - d + 1) % Y
        dst = d if way == 0 else Y - d
        return remote(
            buf.at[src, piece],
            buf.at[dst, piece],
            sems,
            2 * D * X,
            (way * D + d - 1) * X + i,
            right if way == 0 else left,
        )

    def hop(buf, sems, d):
        def one(i, goes):
            for way in (0, 1):
                if d > 1:
                    ring(buf, sems, way, d - 1, i).wait_recv()
                if goes[way]:
                    ring(buf, sems, way, d, i).start()

        if d < D:
            lax.fori_loop(0, X, lambda i, _: (one(i, (True, True)), 0)[1], 0)
        else:
            lax.fori_loop(0, X // 2, lambda i, _: (one(i, (True, False)), 0)[1], 0)
            lax.fori_loop(X // 2, X, lambda i, _: (one(i, (False, True)), 0)[1], 0)

    def enter(buf, sems, copies):
        for i in range(X):
            o = i if (i < 2 or X == 2) else X + 1 - i
            if o:
                copies[o].wait_recv()
            else:
                copies[o].wait()
            for way in (0, 1):
                if D > 1 or (way == 0) == (i < X // 2):
                    ring(buf, sems, way, 1, i).start()

    def last(buf, sems):
        lax.fori_loop(
            0, X // 2, lambda i, _: (ring(buf, sems, 0, D, i).wait_recv(), 0)[1], 0
        )
        lax.fori_loop(
            X // 2, X, lambda i, _: (ring(buf, sems, 1, D, i).wait_recv(), 0)[1], 0
        )

    def drain(buf, sems):
        for d in range(1, D + 1):
            for way in (0, 1):
                lo, hi = (0, X) if d < D else ((0, X // 2) if way == 0 else (X // 2, X))
                lax.fori_loop(
                    lo,
                    hi,
                    lambda i, _, way=way, d=d: (ring(buf, sems, way, d, i).wait_send(), 0)[1],
                    0,
                )

    enter(kb, s_k, k_cp)

    for o in range(X):
        if o:
            q_cp[o].wait_recv()
        else:
            q_cp[o].wait()
    qs_cp = pltpu.make_async_remote_copy(
        src_ref=qb.at[c],
        dst_ref=qb.at[c],
        send_sem=s_q.at[0],
        recv_sem=s_q.at[X],
        device_id=sib,
        device_id_type=MESH,
    )
    qs_cp.start()

    scan(True)
    steps = lax.broadcasted_iota(jnp.int32, (SUB, W), 0).astype(jnp.float32) + 1.0
    for m in range(rates.shape[0]):
        dd[m] = wgt[m : m + 1, :] * jnp.exp(-rates[m : m + 1, :] * steps)

    for k in range(1, Y):
        t_cp[k - 1].wait_recv()
    row_total = fp[Y - 1 - y] * tb[0]
    before = jnp.zeros_like(rates)
    for k in range(1, Y):
        part = tb[k]
        row_total = row_total + fp[Y - 1 - lax.rem(y + Y - k, Y)] * part
        before = before + jnp.where(k <= y, fp[k - 1] * part, 0.0)
    rb[0] = row_total
    r_cp = [
        remote(rb.at[0], rb.at[o], s_r, X, o, seq_id(lax.rem(x + o, X), y, c)) for o in range(1, X)
    ]
    for o in range(1, X):
        r_cp[o - 1].start()

    for d in range(2, min(D, 2) + 1):
        hop(kb, s_k, d)

    for o in range(1, X):
        r_cp[o - 1].wait_recv()
    rows_before = jnp.zeros_like(rates)
    for o in range(1, X):
        fade = jnp.exp((-SPAN * Y * (o - 1)) * rates)
        rows_before = rows_before + jnp.where(o <= x, fade * rb[o], 0.0)
    chip_in = before + fp[y] * rows_before
    carry = jnp.where(c == 0, chip_in, first + f_one * chip_in)

    in_go.wait()
    skip = sg_ref[...]
    for n in range(chains):
        for b in range(SUB // 8):
            r0 = n * SUB + b * 8
            acc = y0[r0 : r0 + 8, :] + skip * g[r0 : r0 + 8, :]
            for m in range(rates.shape[0]):
                acc = acc + dd[m, b * 8 : b * 8 + 8, :] * carry[m : m + 1, :]
            cv[r0 : r0 + 8, :] = go[r0 : r0 + 8, :].astype(jnp.float32) * acc
        carry = ends[n] + d_sub * carry

    squares = jnp.zeros((8, T), jnp.float32)
    for h in range(X):
        block = cv[:, h * HD : (h + 1) * HD].T
        ct[h] = block
        squares = squares + jnp.sum((block * block).reshape(HD // 8, 8, T), axis=0)
    sq[0] = squares
    s_cp = [
        remote(sq.at[0], sq.at[k], s_s, Z, k, {"chan": lax.rem(z + k, Z)}) for k in range(1, Z)
    ]
    for k in sorted(range(1, Z), key=lambda k: -min(k, Z - k)):
        s_cp[k - 1].start()

    to_log2 = math.log2(math.e) / math.sqrt(HD)
    delta = lax.broadcasted_iota(jnp.int32, (T, CORES * T), 0) - lax.broadcasted_iota(
        jnp.int32, (T, CORES * T), 1
    )

    def slot_of(i):
        half = (i + 1) // 2
        return jnp.where(lax.rem(i, 2) == 1, half, lax.rem(Y - half, Y))

    def weigh(j):
        from_y = lax.rem(y + Y - j, Y)
        visible = delta <= (y - from_y) * (CORES * T) - c * T
        for xp in range(X):
            n = (xp + 1) * T
            keys = kb[j, 0 : xp + 1].reshape(n, HD)
            rows = jnp.concatenate([qb[0, xp], qb[1, xp]], axis=0)
            sc = lax.dot_general(
                keys, rows, (((1,), (1,)), ((), ())), preferred_element_type=jnp.float32
            )
            edge = jnp.where(visible, sc[n - T :], NEG)
            top = jnp.max(edge, axis=0, keepdims=True)
            if xp:
                top = jnp.maximum(top, jnp.max(sc[: n - T], axis=0, keepdims=True))
            top = top * to_log2
            ex = jnp.exp2(edge * to_log2 - top)
            tot = jnp.sum(ex, axis=0, keepdims=True)
            pt[j, xp, n - T : n, :] = ex.astype(jnp.bfloat16)
            if xp:
                ex = jnp.exp2(sc[: n - T] * to_log2 - top)
                tot = tot + jnp.sum(ex, axis=0, keepdims=True)
                pt[j, xp, : n - T, :] = ex.astype(jnp.bfloat16)
            ms[j, xp : xp + 1, :] = top
            ls[j, xp : xp + 1, :] = tot

    def weigh_range(a, b):
        lax.fori_loop(a, b, lambda i, _: (weigh(slot_of(i)), 0)[1], 0)

    def mix(j, fresh=False):
        for xp in range(X):
            n = (xp + 1) * T
            vals = jnp.concatenate([vb[j, p] for p in range(xp + 1)], axis=1)
            part = jnp.dot(vals, pt[j, xp, :n, :], preferred_element_type=jnp.float32)
            part = part * ms[j, xp : xp + 1, :]
            for cc in range(CORES):
                piece = part[:, cc * T : (cc + 1) * T]
                if fresh:
                    ac[cc, xp, :HD, :] = piece
                else:
                    ac[cc, xp, :HD, :] += piece

    qs_cp.wait_recv()
    weigh_range(0, 1)
    for d in range(3, min(D, 3) + 1):
        hop(kb, s_k, d)
    ready = min(2 * 1 + 1, Y) if D > 1 else 1
    weigh_range(1, ready)

    for k in range(1, Z):
        s_cp[k - 1].wait_recv()
    squares = sq[0]
    for k in range(1, Z):
        squares = squares + sq[k]
    mean = jnp.sum(squares, axis=0, keepdims=True) / float(W * Z)
    inv = lax.rsqrt(mean + 1e-6)
    for h in range(X):
        vs[h] = (ct[h] * inv).astype(jnp.bfloat16)
    in_v = pltpu.make_async_copy(vs.at[x], vb.at[0, x], s_in.at[5])
    in_v.start()
    v_cp = [x_copy(lambda h: vs.at[h], vb.at[0, x], s_vx, o) if o else in_v for o in range(X)]
    for o in range(1, X):
        v_cp[o].start()
    enter(vb, s_v, v_cp)

    for d in range(4, D + 1):
        hop(kb, s_k, d)
    if D > 2:
        weigh_range(3, 5)
    if D > 2:
        hop(vb, s_v, 2)
    if D > 3:
        weigh_range(5, 7)
    last(kb, s_k)
    weigh_range(Y - 1, Y)

    peak = ms[0]
    for j in range(1, Y):
        peak = jnp.maximum(peak, ms[j])
    tot = jnp.zeros_like(peak)
    for j in range(Y):
        fade = jnp.exp2(ms[j] - peak)
        tot = tot + ls[j] * fade
        ms[j] = fade
    for xp in range(X):
        for cc in range(CORES):
            ac[cc, xp, HD : HD + 1, :] = peak[xp : xp + 1, cc * T : (cc + 1) * T]
            ac[cc, xp, HD + 1 : HD + 2, :] = tot[xp : xp + 1, cc * T : (cc + 1) * T]
            ac[cc, xp, HD + 2 : HD + 8, :] = jnp.zeros((6, T), jnp.float32)

    mix(0, fresh=True)

    def mix_range(a, b):
        lax.fori_loop(a, b, lambda i, _: (mix(slot_of(i)), 0)[1], 0)

    for d in range(2, D + 1):
        if not (d == 2 and D > 2):
            hop(vb, s_v, d)
        if d < D or D == 2:
            pass
        mix_range(2 * d - 3, 2 * d - 1)
    last(vb, s_v)
    mix_range(Y - 1, Y)

    m_cp = [remote(ac.at[1 - c, xp], orx.at[xp], s_m, X, xp, sib) for xp in range(X)]
    for xp in range(X):
        m_cp[xp].start()
    for xp in range(X):
        m_cp[xp].wait_recv()
    out_cp = []
    for o in list(range(1, X)) + [0]:
        xp = lax.rem(x + o, X)
        m0, m1 = ac[c, xp, HD : HD + 1, :], orx[xp, HD : HD + 1, :]
        l0, l1 = ac[c, xp, HD + 1 : HD + 2, :], orx[xp, HD + 1 : HD + 2, :]
        top = jnp.maximum(m0, m1)
        a0, a1 = jnp.exp2(m0 - top), jnp.exp2(m1 - top)
        both = (ac[c, xp, :HD, :] * a0 + orx[xp, :HD, :] * a1) / (l0 * a0 + l1 * a1)
        fs[o] = both.T.astype(jnp.bfloat16)
        if o:
            cp = remote(fs.at[o], o_ref.at[:, cols(x)], s_o, X, o, seq_id(xp, y, c))
        else:
            cp = pltpu.make_async_copy(fs.at[0], o_ref.at[:, cols(x)], s_in.at[6])
        cp.start()
        out_cp.append(cp)

    e_cp.wait_send()
    qs_cp.wait_send()
    for o in range(1, X):
        q_cp[o].wait_send()
        k_cp[o].wait_send()
        v_cp[o].wait_send()
        r_cp[o - 1].wait_send()
    for cp in t_cp + s_cp + m_cp:
        cp.wait_send()
    drain(kb, s_k)
    drain(vb, s_v)
    for cp in out_cp:
        cp.wait()


def local(X, Y, Z, go, gi, vi, pr, pw, sg, q, k):
    T, W = go.shape
    modes = pr.shape[0]
    D = Y // 2
    f32, bf16 = jnp.float32, jnp.bfloat16
    hbm = pl.BlockSpec(memory_space=pl.ANY)
    vmem = pl.BlockSpec(memory_space=pltpu.VMEM)
    dma = lambda n: pltpu.SemaphoreType.DMA((n,))
    return pl.pallas_call(
        functools.partial(kernel, X, Y, Z),
        out_shape=jax.ShapeDtypeStruct((T, W), bf16),
        in_specs=[hbm, hbm, hbm, vmem, vmem, vmem, hbm, hbm],
        out_specs=vmem,
        scratch_shapes=[
            pltpu.VMEM((T, W), bf16),
            pltpu.VMEM((T, W), bf16),
            pltpu.VMEM((T, W), bf16),
            pltpu.VMEM((T, W), f32),
            pltpu.VMEM((T, W), f32),
            pltpu.VMEM((T, W), f32),
            pltpu.VMEM((X, HD, T), f32),
            pltpu.VMEM((modes, SUB, W), f32),
            pltpu.VMEM((Y, modes, W), f32),
            pltpu.VMEM((modes, W), f32),
            pltpu.VMEM((modes, W), f32),
            pltpu.VMEM((Y, modes, W), f32),
            pltpu.VMEM((X, modes, W), f32),
            pltpu.VMEM((Z, 8, T), f32),
            pltpu.VMEM((X, HD, T), bf16),
            pltpu.VMEM((CORES, X, T, HD), bf16),
            pltpu.VMEM((Y, X, T, HD), bf16),
            pltpu.VMEM((Y, X, HD, T), bf16),
            pltpu.VMEM((Y, X, X * T, CORES * T), bf16),
            pltpu.VMEM((Y, X, CORES * T), f32),
            pltpu.VMEM((Y, X, CORES * T), f32),
            pltpu.VMEM((CORES, X, HD + 8, T), f32),
            pltpu.VMEM((X, HD + 8, T), f32),
            pltpu.VMEM((X, T, HD), bf16),
            dma(8),
            dma(2),
            dma(2 * Y),
            dma(2 * X),
            dma(2 * Z),
            dma(2 * X),
            dma(2 * X),
            dma(4 * D * X),
            dma(2 * X),
            dma(4 * D * X),
            dma(2 * X),
            dma(2 * X),
        ],
        compiler_params=pltpu.CompilerParams(
            collective_id=0, has_side_effects=True, vmem_limit_bytes=48 * 1024 * 1024
        ),
    )(go, gi, vi, pr, pw, sg.reshape(1, W), q, k)


def solution(mesh, X=4, Y=8):
    Z = mesh.shape["chan"]
    rows = P("seq", "chan")
    in_specs = (rows, rows, rows, P(None, "chan"), P(None, "chan"), P("chan"), rows, rows)
    return jax.shard_map(
        functools.partial(local, X, Y, Z),
        mesh=mesh,
        in_specs=in_specs,
        out_specs=rows,
        check_vma=False,
    )
```

```python
import functools
import math

import jax
import jax.numpy as jnp
from jax import lax
from jax.experimental import pallas as pl
from jax.experimental.pallas import tpu as pltpu
from jax.sharding import PartitionSpec as P

HD = 128
CORES = 2
SUB = 32
MESH = pl.DeviceIdType.MESH
NEG = -1e30


def kernel(
    X,
    Y,
    Z,
    go_hbm,
    gi_hbm,
    vi_hbm,
    pr_hbm,
    pw_hbm,
    sg_hbm,
    q_hbm,
    k_hbm,
    o_ref,
    pr_ref,
    pw_ref,
    sg_ref,
    go,
    gi,
    vi,
    g,
    y0,
    cv,
    dd,
    fp,
    e_own,
    e_sib,
    tb,
    rb,
    sq,
    rr,
    vs,
    qb,
    kb,
    vb,
    pt,
    ms,
    ls,
    ac,
    orx,
    fs,
    s_in,
    s_e,
    s_t,
    s_r,
    s_s,
    s_rx,
    s_ry,
    s_q,
    s_kx,
    s_k,
    s_vx,
    s_v,
    s_m,
    s_o,
):
    T = go.shape[0]
    W = go.shape[1]
    D = Y // 2
    SPAN = float(CORES * T)
    s = lax.axis_index("seq")
    z = lax.axis_index("chan")
    c = lax.rem(s, CORES)
    chip = s // CORES
    y = lax.rem(chip, Y)
    x = chip // Y

    def seq_id(xx, yy, cc):
        return {"seq": (xx * Y + yy) * CORES + cc}

    sib = {"seq": s + 1 - 2 * c}
    peers = [sib]
    peers += [seq_id(x, lax.rem(y + k, Y), c) for k in range(1, Y)]
    peers += [seq_id(lax.rem(x + o, X), y, c) for o in range(1, X)]
    peers += [{"chan": lax.rem(z + k, Z)} for k in range(1, Z)]

    barrier = pltpu.get_barrier_semaphore()
    for p in peers:
        pl.semaphore_signal(barrier, inc=1, device_id=p, device_id_type=MESH)

    cols = lambda h: pl.ds(pl.multiple_of(h * HD, HD), HD)
    in_gi = pltpu.make_async_copy(gi_hbm, gi, s_in.at[0])
    in_vi = pltpu.make_async_copy(vi_hbm, vi, s_in.at[1])
    in_go = pltpu.make_async_copy(go_hbm, go, s_in.at[2])
    in_q = pltpu.make_async_copy(q_hbm.at[:, cols(x)], qb.at[c, x], s_in.at[3])
    in_k = pltpu.make_async_copy(k_hbm.at[:, cols(x)], kb.at[0, x], s_in.at[4])
    in_pr = pltpu.make_async_copy(pr_hbm, pr_ref, s_in.at[7])
    in_pw = pltpu.make_async_copy(pw_hbm, pw_ref, s_in.at[8])
    in_sg = pltpu.make_async_copy(sg_hbm, sg_ref, s_in.at[9])
    in_gi.start()
    in_vi.start()
    in_pr.start()
    in_pw.start()
    in_sg.start()
    in_go.start()
    in_q.start()
    in_k.start()

    def remote(src, dst, sems, n, i, dev):
        return pltpu.make_async_remote_copy(
            src_ref=src,
            dst_ref=dst,
            send_sem=sems.at[i],
            recv_sem=sems.at[n + i],
            device_id=dev,
            device_id_type=MESH,
        )

    in_pr.wait()
    in_pw.wait()
    rates = pr_ref[...]
    decay = jnp.exp(-rates)
    d_sub = jnp.exp(-float(SUB) * rates)
    wgt = pw_ref[...] * jnp.sqrt(rates)
    chains = T // SUB
    state0 = jnp.zeros(rates.shape, jnp.float32)

    in_gi.wait()
    in_vi.wait()
    g[...] = gi[...].astype(jnp.float32) * vi[...].astype(jnp.float32)

    def scan(emit):
        def body(i, states):
            out = []
            for n in range(chains):
                row = n * SUB + i
                st = decay * states[n] + g[pl.ds(row, 1), :]
                if emit:
                    y0[pl.ds(row, 1), :] = jnp.sum(wgt * st, axis=0, keepdims=True)
                out.append(st)
            return tuple(out)

        return lax.fori_loop(0, SUB, body, (state0,) * chains, unroll=8)

    ends = scan(False)
    total = ends[0]
    for n in range(1, chains):
        total = ends[n] + d_sub * total
    f_one = jnp.exp(-float(T) * rates)
    tb[0] = jnp.where(c == 0, f_one * total, total)

    pl.semaphore_wait(barrier, len(peers))

    t_cp = [
        remote(tb.at[0], tb.at[k], s_t, Y, k, seq_id(x, lax.rem(y + k, Y), c)) for k in range(1, Y)
    ]
    for k in sorted(range(1, Y), key=lambda k: -min(k, Y - k)):
        t_cp[k - 1].start()

    def x_copy(src, dst, sems, o):
        h = lax.rem(x + o, X)
        return remote(src(h), dst, sems, X, o, seq_id(h, y, c))

    q_cp = [
        x_copy(lambda h: q_hbm.at[:, cols(h)], qb.at[c, x], s_q, o) if o else in_q for o in range(X)
    ]
    k_cp = [
        x_copy(lambda h: k_hbm.at[:, cols(h)], kb.at[0, x], s_kx, o) if o else in_k
        for o in range(X)
    ]
    for o in range(1, X):
        k_cp[o].start()
    for o in range(1, X):
        q_cp[o].start()

    right = seq_id(x, lax.rem(y + 1, Y), c)
    left = seq_id(x, lax.rem(y + Y - 1, Y), c)

    def offset(i):
        return jnp.where(i < 2, i, X + 1 - i) if X > 2 else i

    def ring(buf, sems, way, d, i):
        piece = lax.rem(x + X - offset(i), X)
        src = d - 1 if way == 0 else (Y - d + 1) % Y
        dst = d if way == 0 else Y - d
        return remote(
            buf.at[src, piece],
            buf.at[dst, piece],
            sems,
            2 * D * X,
            (way * D + d - 1) * X + i,
            right if way == 0 else left,
        )

    def hop(buf, sems, d):
        def one(i, goes):
            for way in (0, 1):
                if d > 1:
                    ring(buf, sems, way, d - 1, i).wait_recv()
                if goes[way]:
                    ring(buf, sems, way, d, i).start()

        if d < D:
            lax.fori_loop(0, X, lambda i, _: (one(i, (True, True)), 0)[1], 0)
        else:
            lax.fori_loop(0, X // 2, lambda i, _: (one(i, (True, False)), 0)[1], 0)
            lax.fori_loop(X // 2, X, lambda i, _: (one(i, (False, True)), 0)[1], 0)

    def enter(buf, sems, copies, lo, hi):
        for i in range(lo, hi):
            o = i if (i < 2 or X == 2) else X + 1 - i
            if o:
                copies[o].wait_recv()
            else:
                copies[o].wait()
            for way in (0, 1):
                if D > 1 or (way == 0) == (i < X // 2):
                    ring(buf, sems, way, 1, i).start()

    def last(buf, sems):
        lax.fori_loop(
            0, X // 2, lambda i, _: (ring(buf, sems, 0, D, i).wait_recv(), 0)[1], 0
        )
        lax.fori_loop(
            X // 2, X, lambda i, _: (ring(buf, sems, 1, D, i).wait_recv(), 0)[1], 0
        )

    def drain(buf, sems):
        for d in range(1, D + 1):
            for way in (0, 1):
                lo, hi = (0, X) if d < D else ((0, X // 2) if way == 0 else (X // 2, X))
                lax.fori_loop(
                    lo,
                    hi,
                    lambda i, _, way=way, d=d: (ring(buf, sems, way, d, i).wait_send(), 0)[1],
                    0,
                )

    enter(kb, s_k, k_cp, 0, 1)

    scan(True)
    for n in range(Y):
        fp[n] = jnp.exp((-SPAN * n) * rates)
    steps = lax.broadcasted_iota(jnp.int32, (SUB, W), 0).astype(jnp.float32) + 1.0
    for m in range(rates.shape[0]):
        dd[m] = wgt[m : m + 1, :] * jnp.exp(-rates[m : m + 1, :] * steps)

    enter(kb, s_k, k_cp, 1, X)

    for k in range(1, Y):
        t_cp[k - 1].wait_recv()
    row_total = fp[Y - 1 - y] * tb[0]
    before = jnp.zeros_like(rates)
    for k in range(1, Y):
        part = tb[k]
        row_total = row_total + fp[Y - 1 - lax.rem(y + Y - k, Y)] * part
        before = before + jnp.where(k <= y, fp[k - 1] * part, 0.0)
    rb[0] = row_total
    r_cp = [
        remote(rb.at[0], rb.at[o], s_r, X, o, seq_id(lax.rem(x + o, X), y, c)) for o in range(1, X)
    ]
    for o in range(1, X):
        r_cp[o - 1].start()

    for o in range(X):
        if o:
            q_cp[o].wait_recv()
        else:
            q_cp[o].wait()
    qs_cp = pltpu.make_async_remote_copy(
        src_ref=qb.at[c],
        dst_ref=qb.at[c],
        send_sem=s_q.at[0],
        recv_sem=s_q.at[X],
        device_id=sib,
        device_id_type=MESH,
    )
    qs_cp.start()
    for d in range(2, min(D, 2) + 1):
        hop(kb, s_k, d)

    for o in range(1, X):
        r_cp[o - 1].wait_recv()
    rows_before = jnp.zeros_like(rates)
    for o in range(1, X):
        fade = jnp.exp((-SPAN * Y * (o - 1)) * rates)
        rows_before = rows_before + jnp.where(o <= x, fade * rb[o], 0.0)
    part = before + fp[y] * rows_before
    e_own[...] = jnp.where(c == 0, f_one * part + total, part)
    e_cp = remote(e_own, e_sib, s_e, 1, 0, sib)
    e_cp.start()
    e_cp.wait_recv()
    carry = e_sib[...] + jnp.where(c == 0, part, f_one * part)

    in_go.wait()
    in_sg.wait()
    skip = sg_ref[...]
    for n in range(chains):
        for b in range(SUB // 8):
            r0 = n * SUB + b * 8
            acc = y0[r0 : r0 + 8, :] + skip * g[r0 : r0 + 8, :]
            for m in range(rates.shape[0]):
                acc = acc + dd[m, b * 8 : b * 8 + 8, :] * carry[m : m + 1, :]
            cv[r0 : r0 + 8, :] = go[r0 : r0 + 8, :].astype(jnp.float32) * acc
        carry = ends[n] + d_sub * carry

    squares = jnp.zeros((8, T), jnp.float32)
    for h in range(X):
        block = cv[:, h * HD : (h + 1) * HD].T
        vs[h] = block.astype(jnp.bfloat16)
        squares = squares + jnp.sum((block * block).reshape(HD // 8, 8, T), axis=0)
    in_v = pltpu.make_async_copy(vs.at[x], vb.at[0, x], s_in.at[5])
    in_v.start()
    v_cp = [x_copy(lambda h: vs.at[h], vb.at[0, x], s_vx, o) if o else in_v for o in range(X)]
    for o in range(1, X):
        v_cp[o].start()
    sq[0] = jnp.sum(squares, axis=0, keepdims=True)
    s_cp = [
        remote(sq.at[0], sq.at[k], s_s, Z, k, {"chan": lax.rem(z + k, Z)}) for k in range(1, Z)
    ]
    for k in sorted(range(1, Z), key=lambda k: -min(k, Z - k)):
        s_cp[k - 1].start()
    enter(vb, s_v, v_cp, 0, 1)

    to_log2 = math.log2(math.e) / math.sqrt(HD)
    delta = lax.broadcasted_iota(jnp.int32, (T, CORES * T), 0) - lax.broadcasted_iota(
        jnp.int32, (T, CORES * T), 1
    )

    def slot_of(i):
        half = (i + 1) // 2
        return jnp.where(lax.rem(i, 2) == 1, half, lax.rem(Y - half, Y))

    def weigh(j):
        from_y = lax.rem(y + Y - j, Y)
        visible = delta <= (y - from_y) * (CORES * T) - c * T
        for xp in range(X):
            n = (xp + 1) * T
            keys = kb[j, 0 : xp + 1].reshape(n, HD)
            rows = jnp.concatenate([qb[0, xp], qb[1, xp]], axis=0)
            sc = lax.dot_general(
                keys, rows, (((1,), (1,)), ((), ())), preferred_element_type=jnp.float32
            )
            edge = jnp.where(visible, sc[n - T :], NEG)
            top = jnp.max(edge, axis=0, keepdims=True)
            if xp:
                top = jnp.maximum(top, jnp.max(sc[: n - T], axis=0, keepdims=True))
            top = top * to_log2
            ex = jnp.exp2(edge * to_log2 - top)
            tot = jnp.sum(ex, axis=0, keepdims=True)
            pt[j, xp, n - T : n, :] = ex.astype(jnp.bfloat16)
            if xp:
                ex = jnp.exp2(sc[: n - T] * to_log2 - top)
                tot = tot + jnp.sum(ex, axis=0, keepdims=True)
                pt[j, xp, : n - T, :] = ex.astype(jnp.bfloat16)
            ms[j, xp : xp + 1, :] = top
            ls[j, xp : xp + 1, :] = tot

    def weigh_range(a, b):
        lax.fori_loop(a, b, lambda i, _: (weigh(slot_of(i)), 0)[1], 0)

    def mix(j, fresh=False, only=None):
        inv = [rr[j, p] for p in range(X)]
        for xp in range(X) if only is None else (only,):
            n = (xp + 1) * T
            vals = [
                (vb[j, p].astype(jnp.float32) * inv[p]).astype(jnp.bfloat16) for p in range(xp + 1)
            ]
            vals = jnp.concatenate(vals, axis=1)
            part = jnp.dot(vals, pt[j, xp, :n, :], preferred_element_type=jnp.float32)
            part = part * ms[j, xp : xp + 1, :]
            for cc in range(CORES):
                piece = part[:, cc * T : (cc + 1) * T]
                if fresh:
                    ac[cc, xp, :HD, :] = piece
                else:
                    ac[cc, xp, :HD, :] += piece

    def ry(k):
        return remote(rr.at[0], rr.at[k], s_ry, Y, k, seq_id(x, lax.rem(y + k, Y), c))

    qs_cp.wait_recv()
    weigh_range(0, 1)
    for d in range(3, min(D, 3) + 1):
        hop(kb, s_k, d)
    weigh_range(1, 3)
    enter(vb, s_v, v_cp, 1, X)

    for k in range(1, Z):
        s_cp[k - 1].wait_recv()
    squares = sq[0]
    for k in range(1, Z):
        squares = squares + sq[k]
    rr[0, x] = lax.rsqrt(squares / float(W * Z) + 1e-6)
    rx_cp = [
        remote(rr.at[0, x], rr.at[0, x], s_rx, X, o, seq_id(lax.rem(x + o, X), y, c))
        for o in range(1, X)
    ]
    for cp in rx_cp:
        cp.start()

    for d in range(4, D + 1):
        hop(kb, s_k, d)
    if D > 2:
        weigh_range(3, 5)
    for cp in rx_cp:
        cp.wait_recv()
    for k in sorted(range(1, Y), key=lambda k: -min(k, Y - k)):
        ry(k).start()
    if D > 2:
        hop(vb, s_v, 2)
    if D > 3:
        weigh_range(5, 7)
    last(kb, s_k)
    weigh_range(Y - 1, Y)

    peak = ms[0]
    for j in range(1, Y):
        peak = jnp.maximum(peak, ms[j])
    tot = jnp.zeros_like(peak)
    for j in range(Y):
        fade = jnp.exp2(ms[j] - peak)
        tot = tot + ls[j] * fade
        ms[j] = fade
    for xp in range(X):
        for cc in range(CORES):
            ac[cc, xp, HD : HD + 1, :] = peak[xp : xp + 1, cc * T : (cc + 1) * T]
            ac[cc, xp, HD + 1 : HD + 2, :] = tot[xp : xp + 1, cc * T : (cc + 1) * T]
            ac[cc, xp, HD + 2 : HD + 8, :] = jnp.zeros((6, T), jnp.float32)

    if D > 3:
        hop(vb, s_v, 3)
    mix(0, fresh=True)

    def mix_range(a, b):
        def body(i, _):
            j = slot_of(i)
            ry(j).wait_recv()
            mix(j)
            return 0

        lax.fori_loop(a, b, body, 0)

    for d in range(2, D + 1):
        if not ((d == 2 and D > 2) or (d == 3 and D > 3)):
            hop(vb, s_v, d)
        mix_range(2 * d - 3, 2 * d - 1)

    def merge(xp):
        return remote(ac.at[1 - c, xp], orx.at[xp], s_m, X, xp, sib)

    last(vb, s_v)
    ry(D).wait_recv()
    for xp in reversed(range(X)):
        mix(D, only=xp)
        merge(xp).start()
    out_cp = []
    for o in sorted(range(1, X), key=lambda o: -min(o, X - o)) + [0]:
        xp = lax.rem(x + o, X)
        merge(xp).wait_recv()
        m0, m1 = ac[c, xp, HD : HD + 1, :], orx[xp, HD : HD + 1, :]
        l0, l1 = ac[c, xp, HD + 1 : HD + 2, :], orx[xp, HD + 1 : HD + 2, :]
        top = jnp.maximum(m0, m1)
        a0, a1 = jnp.exp2(m0 - top), jnp.exp2(m1 - top)
        both = (ac[c, xp, :HD, :] * a0 + orx[xp, :HD, :] * a1) / (l0 * a0 + l1 * a1)
        fs[o] = both.T.astype(jnp.bfloat16)
        if o:
            cp = remote(fs.at[o], o_ref.at[:, cols(x)], s_o, X, o, seq_id(xp, y, c))
        else:
            cp = pltpu.make_async_copy(fs.at[0], o_ref.at[:, cols(x)], s_in.at[6])
        cp.start()
        out_cp.append(cp)

    e_cp.wait_send()
    qs_cp.wait_send()
    for o in range(1, X):
        q_cp[o].wait_send()
        k_cp[o].wait_send()
        v_cp[o].wait_send()
        r_cp[o - 1].wait_send()
    for cp in t_cp + s_cp + rx_cp:
        cp.wait_send()
    for xp in range(X):
        merge(xp).wait_send()
    for k in range(1, Y):
        ry(k).wait_send()
    drain(kb, s_k)
    drain(vb, s_v)
    for cp in out_cp:
        cp.wait()


def local(X, Y, Z, go, gi, vi, pr, pw, sg, q, k):
    T, W = go.shape
    modes = pr.shape[0]
    D = Y // 2
    f32, bf16 = jnp.float32, jnp.bfloat16
    hbm = pl.BlockSpec(memory_space=pl.ANY)
    vmem = pl.BlockSpec(memory_space=pltpu.VMEM)
    dma = lambda n: pltpu.SemaphoreType.DMA((n,))
    return pl.pallas_call(
        functools.partial(kernel, X, Y, Z),
        out_shape=jax.ShapeDtypeStruct((T, W), bf16),
        in_specs=[hbm] * 8,
        out_specs=vmem,
        scratch_shapes=[
            pltpu.VMEM((modes, W), f32),
            pltpu.VMEM((modes, W), f32),
            pltpu.VMEM((1, W), f32),
            pltpu.VMEM((T, W), bf16),
            pltpu.VMEM((T, W), bf16),
            pltpu.VMEM((T, W), bf16),
            pltpu.VMEM((T, W), f32),
            pltpu.VMEM((T, W), f32),
            pltpu.VMEM((T, W), f32),
            pltpu.VMEM((modes, SUB, W), f32),
            pltpu.VMEM((Y, modes, W), f32),
            pltpu.VMEM((modes, W), f32),
            pltpu.VMEM((modes, W), f32),
            pltpu.VMEM((Y, modes, W), f32),
            pltpu.VMEM((X, modes, W), f32),
            pltpu.VMEM((Z, 1, T), f32),
            pltpu.VMEM((Y, X, 1, T), f32),
            pltpu.VMEM((X, HD, T), bf16),
            pltpu.VMEM((CORES, X, T, HD), bf16),
            pltpu.VMEM((Y, X, T, HD), bf16),
            pltpu.VMEM((Y, X, HD, T), bf16),
            pltpu.VMEM((Y, X, X * T, CORES * T), bf16),
            pltpu.VMEM((Y, X, CORES * T), f32),
            pltpu.VMEM((Y, X, CORES * T), f32),
            pltpu.VMEM((CORES, X, HD + 8, T), f32),
            pltpu.VMEM((X, HD + 8, T), f32),
            pltpu.VMEM((X, T, HD), bf16),
            dma(10),
            dma(2),
            dma(2 * Y),
            dma(2 * X),
            dma(2 * Z),
            dma(2 * X),
            dma(2 * Y),
            dma(2 * X),
            dma(2 * X),
            dma(4 * D * X),
            dma(2 * X),
            dma(4 * D * X),
            dma(2 * X),
            dma(2 * X),
        ],
        compiler_params=pltpu.CompilerParams(
            collective_id=0, has_side_effects=True, vmem_limit_bytes=67043328
        ),
    )(go, gi, vi, pr, pw, sg.reshape(1, W), q, k)


def solution(mesh, X=4, Y=8):
    Z = mesh.shape["chan"]
    rows = P("seq", "chan")
    in_specs = (rows, rows, rows, P(None, "chan"), P(None, "chan"), P("chan"), rows, rows)
    return jax.shard_map(
        functools.partial(local, X, Y, Z),
        mesh=mesh,
        in_specs=in_specs,
        out_specs=rows,
        check_vma=False,
    )
```

```python
import functools
import math

import jax
import jax.numpy as jnp
from jax import lax
from jax.experimental import pallas as pl
from jax.experimental.pallas import tpu as pltpu
from jax.sharding import PartitionSpec as P

HD = 128
CORES = 2
SUB = 32
MESH = pl.DeviceIdType.MESH
NEG = -1e30


def kernel(
    X,
    Y,
    Z,
    go_hbm,
    gi_hbm,
    vi_hbm,
    pr_hbm,
    pw_hbm,
    sg_hbm,
    q_hbm,
    k_hbm,
    o_ref,
    pr_ref,
    pw_ref,
    sg_ref,
    go,
    gi,
    vi,
    g,
    y0,
    cv,
    dd,
    fp,
    e_own,
    e_sib,
    tb,
    rb,
    sq,
    rr,
    vs,
    qb,
    kb,
    vb,
    pt,
    ms,
    ls,
    ac,
    orx,
    fs,
    s_in,
    s_e,
    s_t,
    s_r,
    s_s,
    s_ry,
    s_q,
    s_kx,
    s_k,
    s_vx,
    s_v,
    s_m,
    s_o,
):
    T = go.shape[0]
    W = go.shape[1]
    D = Y // 2
    SPAN = float(CORES * T)
    s = lax.axis_index("seq")
    z = lax.axis_index("chan")
    c = lax.rem(s, CORES)
    chip = s // CORES
    y = lax.rem(chip, Y)
    x = chip // Y

    def seq_id(xx, yy, cc):
        return {"seq": (xx * Y + yy) * CORES + cc}

    sib = {"seq": s + 1 - 2 * c}
    peers = [sib]
    peers += [{"chan": lax.rem(z + k, Z)} for k in range(1, Z)]
    peers += [
        seq_id(lax.rem(x + n % X, X), lax.rem(y + n // X, Y), c) for n in range(1, X * Y)
    ]

    cols = lambda h: pl.ds(pl.multiple_of(h * HD, HD), HD)
    in_gi = pltpu.make_async_copy(gi_hbm, gi, s_in.at[0])
    in_vi = pltpu.make_async_copy(vi_hbm, vi, s_in.at[1])
    in_go = pltpu.make_async_copy(go_hbm, go, s_in.at[2])
    in_q = pltpu.make_async_copy(q_hbm.at[:, cols(x)], qb.at[c, x], s_in.at[3])
    in_k = pltpu.make_async_copy(k_hbm.at[:, cols(x)], kb.at[0, x], s_in.at[4])
    in_pr = pltpu.make_async_copy(pr_hbm, pr_ref, s_in.at[7])
    in_pw = pltpu.make_async_copy(pw_hbm, pw_ref, s_in.at[8])
    in_sg = pltpu.make_async_copy(sg_hbm, sg_ref, s_in.at[9])
    in_gi.start()
    in_vi.start()
    in_pr.start()
    in_pw.start()
    in_sg.start()
    in_go.start()
    in_q.start()
    in_k.start()

    barrier = pltpu.get_barrier_semaphore()
    for p in peers:
        pl.semaphore_signal(barrier, inc=1, device_id=p, device_id_type=MESH)

    def remote(src, dst, sems, n, i, dev):
        return pltpu.make_async_remote_copy(
            src_ref=src,
            dst_ref=dst,
            send_sem=sems.at[i],
            recv_sem=sems.at[n + i],
            device_id=dev,
            device_id_type=MESH,
        )

    in_pr.wait()
    in_pw.wait()
    rates = pr_ref[...]
    decay = jnp.exp(-rates)
    d_sub = jnp.exp(-float(SUB) * rates)
    wgt = pw_ref[...] * jnp.sqrt(rates)
    chains = T // SUB
    state0 = jnp.zeros(rates.shape, jnp.float32)

    in_gi.wait()
    in_vi.wait()
    g[...] = gi[...].astype(jnp.float32) * vi[...].astype(jnp.float32)

    def scan(emit):
        def body(i, states):
            out = []
            for n in range(chains):
                row = n * SUB + i
                st = decay * states[n] + g[pl.ds(row, 1), :]
                if emit:
                    y0[pl.ds(row, 1), :] = jnp.sum(wgt * st, axis=0, keepdims=True)
                out.append(st)
            return tuple(out)

        return lax.fori_loop(0, SUB, body, (state0,) * chains, unroll=8)

    ends = scan(False)
    total = ends[0]
    for n in range(1, chains):
        total = ends[n] + d_sub * total
    f_one = jnp.exp(-float(T) * rates)
    tb[0] = jnp.where(c == 0, f_one * total, total)

    pl.semaphore_wait(barrier, len(peers))

    t_cp = [
        remote(tb.at[0], tb.at[k], s_t, Y, k, seq_id(x, lax.rem(y + k, Y), c)) for k in range(1, Y)
    ]
    for k in sorted(range(1, Y), key=lambda k: -min(k, Y - k)):
        t_cp[k - 1].start()

    def x_copy(src, dst, sems, o):
        h = lax.rem(x + o, X)
        return remote(src(h), dst, sems, X, o, seq_id(h, y, c))

    q_cp = [
        x_copy(lambda h: q_hbm.at[:, cols(h)], qb.at[c, x], s_q, o) if o else in_q for o in range(X)
    ]
    right = seq_id(x, lax.rem(y + 1, Y), c)
    left = seq_id(x, lax.rem(y + Y - 1, Y), c)

    def offset(i):
        return jnp.where(i < 2, i, X + 1 - i) if X > 2 else i

    def ring(buf, sems, way, d, i):
        piece = lax.rem(x + X - offset(i), X)
        start = min(d - 1, 2)
        far = d - start
        if way == 0:
            src, dst, to = start, d, lax.rem(y + far, Y)
        else:
            src, dst, to = (Y - start) % Y, Y - d, lax.rem(y + Y - far, Y)
        return remote(
            buf.at[src, piece],
            buf.at[dst, piece],
            sems,
            2 * D * X,
            (way * D + d - 1) * X + i,
            seq_id(x, to, c),
        )

    def span(way, d):
        if d < D:
            return 0, X
        return (0, X // 2) if way == 0 else (X // 2, X)

    def each(d, act):
        for way in (0, 1):
            lax.fori_loop(*span(way, d), lambda i, _, way=way: (act(way, i), 0)[1], 0)

    def hop(buf, sems, d, lo=0, hi=X):
        def one(i, goes):
            for way in (0, 1):
                ring(buf, sems, way, d - 1, i).wait_recv()
                for to in (4, 3) if d == 3 else (d,):
                    if to < D or (to == D and goes[way]):
                        ring(buf, sems, way, to, i).start()

        for a, b, goes in ((0, X // 2, (True, False)), (X // 2, X, (False, True))):
            a, b = max(a, lo), min(b, hi)
            if a < b and d <= D:
                lax.fori_loop(a, b, lambda i, _, goes=goes: (one(i, goes), 0)[1], 0)

    def got(buf, sems, d):
        each(d, lambda way, i: ring(buf, sems, way, d, i).wait_recv())

    def drain(buf, sems):
        for d in range(1, D + 1):
            each(d, lambda way, i, d=d: ring(buf, sems, way, d, i).wait_send())

    def inject(src, own, buf, sx, sems):
        far = sorted(range(1, X), key=lambda o: -min(o, X - o))
        copies = [own]

        def beside(o):
            i = o if (o < 2 or X == 2) else X + 1 - o
            h = lax.rem(x + o, X)
            for way, step, slot in ((0, 1, 1), (1, Y - 1, Y - 1)):
                cp = remote(
                    src(h),
                    buf.at[slot, x],
                    sems,
                    2 * D * X,
                    way * D * X + i,
                    seq_id(h, lax.rem(y + step, Y), c),
                )
                cp.start()

        for o in [0] + far:
            beside(o)
        for o in range(1, X):
            copies.append(x_copy(src, buf.at[0, x], sx, o))
        for o in far:
            copies[o].start()
        return copies

    def entered(copies):
        copies[0].wait()
        for cp in copies[1:]:
            cp.wait_recv()

    k_cp = [in_k] + [
        x_copy(lambda h: k_hbm.at[:, cols(h)], kb.at[0, x], s_kx, o) for o in range(1, X)
    ]
    for o in range(1, X):
        k_cp[o].start()

    def enter(lo, hi):
        for i in range(lo, hi):
            o = i if (i < 2 or X == 2) else X + 1 - i
            if o:
                k_cp[o].wait_recv()
            else:
                k_cp[o].wait()
            for way in (0, 1):
                ring(kb, s_k, way, 1, i).start()

    enter(0, 1)
    for o in range(1, X):
        q_cp[o].start()

    scan(True)
    for n in range(Y):
        fp[n] = jnp.exp((-SPAN * n) * rates)
    steps = lax.broadcasted_iota(jnp.int32, (SUB, W), 0).astype(jnp.float32) + 1.0
    for m in range(rates.shape[0]):
        dd[m] = wgt[m : m + 1, :] * jnp.exp(-rates[m : m + 1, :] * steps)

    enter(1, X)

    for k in range(1, Y):
        t_cp[k - 1].wait_recv()
    row_total = fp[Y - 1 - y] * tb[0]
    before = jnp.zeros_like(rates)
    for k in range(1, Y):
        part = tb[k]
        row_total = row_total + fp[Y - 1 - lax.rem(y + Y - k, Y)] * part
        before = before + jnp.where(k <= y, fp[k - 1] * part, 0.0)
    rb[0] = row_total
    r_cp = [
        remote(rb.at[0], rb.at[o], s_r, X, o, seq_id(lax.rem(x + o, X), y, c)) for o in range(1, X)
    ]
    for o in range(1, X):
        r_cp[o - 1].start()

    for o in range(X):
        if o:
            q_cp[o].wait_recv()
        else:
            q_cp[o].wait()
    qs_cp = pltpu.make_async_remote_copy(
        src_ref=qb.at[c],
        dst_ref=qb.at[c],
        send_sem=s_q.at[0],
        recv_sem=s_q.at[X],
        device_id=sib,
        device_id_type=MESH,
    )
    qs_cp.start()
    hop(kb, s_k, 2)

    for o in range(1, X):
        r_cp[o - 1].wait_recv()
    rows_before = jnp.zeros_like(rates)
    for o in range(1, X):
        fade = jnp.exp((-SPAN * Y * (o - 1)) * rates)
        rows_before = rows_before + jnp.where(o <= x, fade * rb[o], 0.0)
    part = before + fp[y] * rows_before
    e_own[...] = jnp.where(c == 0, f_one * part + total, part)
    e_cp = remote(e_own, e_sib, s_e, 1, 0, sib)
    e_cp.start()
    e_cp.wait_recv()
    carry = e_sib[...] + jnp.where(c == 0, part, f_one * part)

    in_go.wait()
    in_sg.wait()
    skip = sg_ref[...]
    for n in range(chains):
        for b in range(SUB // 8):
            r0 = n * SUB + b * 8
            acc = y0[r0 : r0 + 8, :] + skip * g[r0 : r0 + 8, :]
            for m in range(rates.shape[0]):
                acc = acc + dd[m, b * 8 : b * 8 + 8, :] * carry[m : m + 1, :]
            cv[r0 : r0 + 8, :] = go[r0 : r0 + 8, :].astype(jnp.float32) * acc
        carry = ends[n] + d_sub * carry

    squares = jnp.zeros((8, T), jnp.float32)
    for h in range(X):
        block = cv[:, h * HD : (h + 1) * HD].T
        vs[h] = block.astype(jnp.bfloat16)
        squares = squares + jnp.sum((block * block).reshape(HD // 8, 8, T), axis=0)
    in_v = pltpu.make_async_copy(vs.at[x], vb.at[0, x], s_in.at[5])
    in_v.start()
    v_cp = inject(lambda h: vs.at[h], in_v, vb, s_vx, s_v)
    sq[0] = jnp.sum(squares, axis=0, keepdims=True)
    s_cp = [
        remote(sq.at[0], sq.at[k], s_s, Z, k, {"chan": lax.rem(z + k, Z)}) for k in range(1, Z)
    ]
    for k in sorted(range(1, Z), key=lambda k: -min(k, Z - k)):
        s_cp[k - 1].start()

    to_log2 = math.log2(math.e) / math.sqrt(HD)
    delta = lax.broadcasted_iota(jnp.int32, (T, CORES * T), 0) - lax.broadcasted_iota(
        jnp.int32, (T, CORES * T), 1
    )

    def slot_of(i):
        half = (i + 1) // 2
        return jnp.where(lax.rem(i, 2) == 1, half, lax.rem(Y - half, Y))

    def weigh(j):
        from_y = lax.rem(y + Y - j, Y)
        visible = delta <= (y - from_y) * (CORES * T) - c * T
        for xp in range(X):
            n = (xp + 1) * T
            keys = kb[j, 0 : xp + 1].reshape(n, HD)
            rows = jnp.concatenate([qb[0, xp], qb[1, xp]], axis=0)
            sc = lax.dot_general(
                keys, rows, (((1,), (1,)), ((), ())), preferred_element_type=jnp.float32
            )
            edge = jnp.where(visible, sc[n - T :], NEG)
            top = jnp.max(edge, axis=0, keepdims=True)
            if xp:
                top = jnp.maximum(top, jnp.max(sc[: n - T], axis=0, keepdims=True))
            top = top * to_log2
            ex = jnp.exp2(edge * to_log2 - top)
            tot = jnp.sum(ex, axis=0, keepdims=True)
            pt[j, xp, n - T : n, :] = ex.astype(jnp.bfloat16)
            if xp:
                ex = jnp.exp2(sc[: n - T] * to_log2 - top)
                tot = tot + jnp.sum(ex, axis=0, keepdims=True)
                pt[j, xp, : n - T, :] = ex.astype(jnp.bfloat16)
            ms[j, xp : xp + 1, :] = top
            ls[j, xp : xp + 1, :] = tot

    def weigh_range(a, b):
        lax.fori_loop(a, b, lambda i, _: (weigh(slot_of(i)), 0)[1], 0)

    def mix(j, fresh=False, only=None):
        inv = [rr[j, p] for p in range(X)]
        for xp in range(X) if only is None else (only,):
            n = (xp + 1) * T
            vals = [
                (vb[j, p].astype(jnp.float32) * inv[p]).astype(jnp.bfloat16) for p in range(xp + 1)
            ]
            vals = jnp.concatenate(vals, axis=1)
            part = jnp.dot(vals, pt[j, xp, :n, :], preferred_element_type=jnp.float32)
            part = part * ms[j, xp : xp + 1, :]
            for cc in range(CORES):
                piece = part[:, cc * T : (cc + 1) * T]
                if fresh:
                    ac[cc, xp, :HD, :] = piece
                else:
                    ac[cc, xp, :HD, :] += piece

    def ry(n):
        dx, dy = lax.rem(n, X), n // X
        to = seq_id(lax.rem(x + dx, X), lax.rem(y + dy, Y), c)
        return remote(rr.at[0, x], rr.at[dy, x], s_ry, X * Y, n, to)

    def scales(j, lo=0):
        for dx in range(lo, X):
            ry(j * X + dx).wait_recv()

    qs_cp.wait_recv()
    weigh_range(0, 1)
    hop(kb, s_k, 3)
    weigh_range(1, 3)
    hop(vb, s_v, 2, 0, X // 2)

    for k in range(1, Z):
        s_cp[k - 1].wait_recv()
    squares = sq[0]
    for k in range(1, Z):
        squares = squares + sq[k]
    rr[0, x] = lax.rsqrt(squares / float(W * Z) + 1e-6)
    lax.fori_loop(1, X * Y, lambda n, _: (ry(n).start(), 0)[1], 0)

    hop(vb, s_v, 2, X // 2, X)
    if D > 2:
        weigh_range(3, 5)
        hop(vb, s_v, 3)
        got(kb, s_k, 3)
    got(kb, s_k, D)
    weigh_range(5 if D > 2 else 3, Y)

    peak = ms[0]
    for j in range(1, Y):
        peak = jnp.maximum(peak, ms[j])
    tot = jnp.zeros_like(peak)
    for j in range(Y):
        fade = jnp.exp2(ms[j] - peak)
        tot = tot + ls[j] * fade
        ms[j] = fade
    for xp in range(X):
        for cc in range(CORES):
            ac[cc, xp, HD : HD + 1, :] = peak[xp : xp + 1, cc * T : (cc + 1) * T]
            ac[cc, xp, HD + 1 : HD + 2, :] = tot[xp : xp + 1, cc * T : (cc + 1) * T]
            ac[cc, xp, HD + 2 : HD + 8, :] = jnp.zeros((6, T), jnp.float32)

    entered(v_cp)
    scales(0, 1)
    mix(0, fresh=True)

    def mix_range(a, b):
        def body(i, _):
            j = slot_of(i)
            scales(j)
            mix(j)
            return 0

        lax.fori_loop(a, b, body, 0)

    if D > 2:
        mix_range(1, 5)
        got(vb, s_v, 3)
        mix_range(5, 7)
    else:
        mix_range(1, 3)

    def merge(xp):
        return remote(ac.at[1 - c, xp], orx.at[xp], s_m, X, xp, sib)

    got(vb, s_v, D)
    scales(D)
    for xp in reversed(range(X)):
        mix(D, only=xp)
        merge(xp).start()
    out_cp = []
    for o in sorted(range(1, X), key=lambda o: -min(o, X - o)) + [0]:
        xp = lax.rem(x + o, X)
        merge(xp).wait_recv()
        m0, m1 = ac[c, xp, HD : HD + 1, :], orx[xp, HD : HD + 1, :]
        l0, l1 = ac[c, xp, HD + 1 : HD + 2, :], orx[xp, HD + 1 : HD + 2, :]
        top = jnp.maximum(m0, m1)
        a0, a1 = jnp.exp2(m0 - top), jnp.exp2(m1 - top)
        both = (ac[c, xp, :HD, :] * a0 + orx[xp, :HD, :] * a1) / (l0 * a0 + l1 * a1)
        fs[o] = both.T.astype(jnp.bfloat16)
        if o:
            cp = remote(fs.at[o], o_ref.at[:, cols(x)], s_o, X, o, seq_id(xp, y, c))
        else:
            cp = pltpu.make_async_copy(fs.at[0], o_ref.at[:, cols(x)], s_in.at[6])
        cp.start()
        out_cp.append(cp)

    e_cp.wait_send()
    qs_cp.wait_send()
    for o in range(1, X):
        q_cp[o].wait_send()
        k_cp[o].wait_send()
        v_cp[o].wait_send()
        r_cp[o - 1].wait_send()
    for cp in t_cp + s_cp:
        cp.wait_send()
    for xp in range(X):
        merge(xp).wait_send()
    lax.fori_loop(1, X * Y, lambda n, _: (ry(n).wait_send(), 0)[1], 0)
    drain(kb, s_k)
    drain(vb, s_v)
    for cp in out_cp:
        cp.wait()


def local(X, Y, Z, go, gi, vi, pr, pw, sg, q, k):
    T, W = go.shape
    modes = pr.shape[0]
    D = Y // 2
    f32, bf16 = jnp.float32, jnp.bfloat16
    hbm = pl.BlockSpec(memory_space=pl.ANY)
    vmem = pl.BlockSpec(memory_space=pltpu.VMEM)
    dma = lambda n: pltpu.SemaphoreType.DMA((n,))
    return pl.pallas_call(
        functools.partial(kernel, X, Y, Z),
        out_shape=jax.ShapeDtypeStruct((T, W), bf16),
        in_specs=[hbm] * 8,
        out_specs=vmem,
        scratch_shapes=[
            pltpu.VMEM((modes, W), f32),
            pltpu.VMEM((modes, W), f32),
            pltpu.VMEM((1, W), f32),
            pltpu.VMEM((T, W), bf16),
            pltpu.VMEM((T, W), bf16),
            pltpu.VMEM((T, W), bf16),
            pltpu.VMEM((T, W), f32),
            pltpu.VMEM((T, W), f32),
            pltpu.VMEM((T, W), f32),
            pltpu.VMEM((modes, SUB, W), f32),
            pltpu.VMEM((Y, modes, W), f32),
            pltpu.VMEM((modes, W), f32),
            pltpu.VMEM((modes, W), f32),
            pltpu.VMEM((Y, modes, W), f32),
            pltpu.VMEM((X, modes, W), f32),
            pltpu.VMEM((Z, 1, T), f32),
            pltpu.VMEM((Y, X, 1, T), f32),
            pltpu.VMEM((X, HD, T), bf16),
            pltpu.VMEM((CORES, X, T, HD), bf16),
            pltpu.VMEM((Y, X, T, HD), bf16),
            pltpu.VMEM((Y, X, HD, T), bf16),
            pltpu.VMEM((Y, X, X * T, CORES * T), bf16),
            pltpu.VMEM((Y, X, CORES * T), f32),
            pltpu.VMEM((Y, X, CORES * T), f32),
            pltpu.VMEM((CORES, X, HD + 8, T), f32),
            pltpu.VMEM((X, HD + 8, T), f32),
            pltpu.VMEM((X, T, HD), bf16),
            dma(10),
            dma(2),
            dma(2 * Y),
            dma(2 * X),
            dma(2 * Z),
            dma(2 * X * Y),
            dma(2 * X),
            dma(2 * X),
            dma(4 * D * X),
            dma(2 * X),
            dma(4 * D * X),
            dma(2 * X),
            dma(2 * X),
        ],
        compiler_params=pltpu.CompilerParams(
            collective_id=0, has_side_effects=True, vmem_limit_bytes=67043328
        ),
    )(go, gi, vi, pr, pw, sg.reshape(1, W), q, k)


def solution(mesh, X=4, Y=8):
    Z = mesh.shape["chan"]
    rows = P("seq", "chan")
    in_specs = (rows, rows, rows, P(None, "chan"), P(None, "chan"), P("chan"), rows, rows)
    return jax.shard_map(
        functools.partial(local, X, Y, Z),
        mesh=mesh,
        in_specs=in_specs,
        out_specs=rows,
        check_vma=False,
    )
```

```python
import functools
import math

import jax
import jax.numpy as jnp
from jax import lax
from jax.experimental import pallas as pl
from jax.experimental.pallas import tpu as pltpu
from jax.sharding import PartitionSpec as P

HD = 128
CORES = 2
SUB = 32
MESH = pl.DeviceIdType.MESH
NEG = -1e30


def kernel(
    X,
    Y,
    Z,
    go_hbm,
    gi_hbm,
    vi_hbm,
    pr_hbm,
    pw_hbm,
    sg_hbm,
    q_hbm,
    k_hbm,
    o_ref,
    pr_ref,
    pw_ref,
    sg_ref,
    go,
    gi,
    vi,
    g,
    y0,
    cv,
    dd,
    fp,
    e_own,
    e_sib,
    tb,
    rb,
    sq,
    rr,
    vs,
    qb,
    kb,
    vb,
    pt,
    ms,
    ls,
    ac,
    orx,
    fs,
    s_in,
    s_e,
    s_t,
    s_r,
    s_s,
    s_ry,
    s_q,
    s_kx,
    s_k,
    s_vx,
    s_v,
    s_m,
    s_o,
):
    T = go.shape[0]
    W = go.shape[1]
    D = Y // 2
    SPAN = float(CORES * T)
    s = lax.axis_index("seq")
    z = lax.axis_index("chan")
    c = lax.rem(s, CORES)
    chip = s // CORES
    y = lax.rem(chip, Y)
    x = chip // Y

    def seq_id(xx, yy, cc):
        return {"seq": (xx * Y + yy) * CORES + cc}

    sib = {"seq": s + 1 - 2 * c}
    peers = [sib]
    peers += [{"chan": lax.rem(z + k, Z)} for k in range(1, Z)]
    peers += [
        seq_id(lax.rem(x + n % X, X), lax.rem(y + n // X, Y), c) for n in range(1, X * Y)
    ]

    cols = lambda h: pl.ds(pl.multiple_of(h * HD, HD), HD)
    in_gi = pltpu.make_async_copy(gi_hbm, gi, s_in.at[0])
    in_vi = pltpu.make_async_copy(vi_hbm, vi, s_in.at[1])
    in_go = pltpu.make_async_copy(go_hbm, go, s_in.at[2])
    in_q = pltpu.make_async_copy(q_hbm.at[:, cols(x)], qb.at[c, x], s_in.at[3])
    in_k = pltpu.make_async_copy(k_hbm.at[:, cols(x)], kb.at[0, x], s_in.at[4])
    in_pr = pltpu.make_async_copy(pr_hbm, pr_ref, s_in.at[7])
    in_pw = pltpu.make_async_copy(pw_hbm, pw_ref, s_in.at[8])
    in_sg = pltpu.make_async_copy(sg_hbm, sg_ref, s_in.at[9])
    in_gi.start()
    in_vi.start()
    in_pr.start()
    in_pw.start()
    in_sg.start()
    in_go.start()
    in_q.start()
    in_k.start()

    barrier = pltpu.get_barrier_semaphore()
    for p in peers:
        pl.semaphore_signal(barrier, inc=1, device_id=p, device_id_type=MESH)

    def remote(src, dst, sems, n, i, dev):
        return pltpu.make_async_remote_copy(
            src_ref=src,
            dst_ref=dst,
            send_sem=sems.at[i],
            recv_sem=sems.at[n + i],
            device_id=dev,
            device_id_type=MESH,
        )

    in_pr.wait()
    in_pw.wait()
    rates = pr_ref[...]
    decay = jnp.exp(-rates)
    d_sub = jnp.exp(-float(SUB) * rates)
    wgt = pw_ref[...] * jnp.sqrt(rates)
    chains = T // SUB
    state0 = jnp.zeros(rates.shape, jnp.float32)

    in_gi.wait()
    in_vi.wait()
    g[...] = gi[...].astype(jnp.float32) * vi[...].astype(jnp.float32)

    def scan(emit):
        def body(i, states):
            out = []
            for n in range(chains):
                row = n * SUB + i
                st = decay * states[n] + g[pl.ds(row, 1), :]
                if emit:
                    y0[pl.ds(row, 1), :] = jnp.sum(wgt * st, axis=0, keepdims=True)
                out.append(st)
            return tuple(out)

        return lax.fori_loop(0, SUB, body, (state0,) * chains, unroll=8)

    ends = scan(False)
    total = ends[0]
    for n in range(1, chains):
        total = ends[n] + d_sub * total
    f_one = jnp.exp(-float(T) * rates)
    tb[0] = jnp.where(c == 0, f_one * total, total)

    pl.semaphore_wait(barrier, len(peers))

    t_cp = [
        remote(tb.at[0], tb.at[k], s_t, Y, k, seq_id(x, lax.rem(y + k, Y), c)) for k in range(1, Y)
    ]
    for k in sorted(range(1, Y), key=lambda k: -min(k, Y - k)):
        t_cp[k - 1].start()

    def x_copy(src, dst, sems, o):
        h = lax.rem(x + o, X)
        return remote(src(h), dst, sems, X, o, seq_id(h, y, c))

    q_cp = [
        x_copy(lambda h: q_hbm.at[:, cols(h)], qb.at[c, x], s_q, o) if o else in_q for o in range(X)
    ]
    right = seq_id(x, lax.rem(y + 1, Y), c)
    left = seq_id(x, lax.rem(y + Y - 1, Y), c)

    def offset(i):
        return jnp.where(i < 2, i, X + 1 - i) if X > 2 else i

    def ring(buf, sems, way, d, i):
        piece = lax.rem(x + X - offset(i), X)
        start = min(d - 1, 2) if buf is vb else d - 1
        far = d - start
        if way == 0:
            src, dst, to = start, d, lax.rem(y + far, Y)
        else:
            src, dst, to = (Y - start) % Y, Y - d, lax.rem(y + Y - far, Y)
        return remote(
            buf.at[src, piece],
            buf.at[dst, piece],
            sems,
            2 * D * X,
            (way * D + d - 1) * X + i,
            seq_id(x, to, c),
        )

    def span(way, d):
        if d < D:
            return 0, X
        return (0, X // 2) if way == 0 else (X // 2, X)

    def each(d, act):
        for way in (0, 1):
            lax.fori_loop(*span(way, d), lambda i, _, way=way: (act(way, i), 0)[1], 0)

    def hop(buf, sems, d, lo=0, hi=X):
        def one(i, goes):
            for way in (0, 1):
                ring(buf, sems, way, d - 1, i).wait_recv()
                for to in (4, 3) if d == 3 and buf is vb else (d,):
                    if to < D or (to == D and goes[way]):
                        ring(buf, sems, way, to, i).start()

        for a, b, goes in ((0, X // 2, (True, False)), (X // 2, X, (False, True))):
            a, b = max(a, lo), min(b, hi)
            if a < b and d <= D:
                lax.fori_loop(a, b, lambda i, _, goes=goes: (one(i, goes), 0)[1], 0)

    def got(buf, sems, d):
        each(d, lambda way, i: ring(buf, sems, way, d, i).wait_recv())

    def drain(buf, sems):
        for d in range(1, D + 1):
            each(d, lambda way, i, d=d: ring(buf, sems, way, d, i).wait_send())

    def inject(src, own, buf, sx, sems):
        far = sorted(range(1, X), key=lambda o: -min(o, X - o))
        copies = [own]

        def beside(o):
            i = o if (o < 2 or X == 2) else X + 1 - o
            h = lax.rem(x + o, X)
            for way, step, slot in ((0, 1, 1), (1, Y - 1, Y - 1)):
                cp = remote(
                    src(h),
                    buf.at[slot, x],
                    sems,
                    2 * D * X,
                    way * D * X + i,
                    seq_id(h, lax.rem(y + step, Y), c),
                )
                cp.start()

        for o in [0] + far:
            beside(o)
        for o in range(1, X):
            copies.append(x_copy(src, buf.at[0, x], sx, o))
        for o in far:
            copies[o].start()
        return copies

    def entered(copies):
        copies[0].wait()
        for cp in copies[1:]:
            cp.wait_recv()

    k_cp = [in_k] + [
        x_copy(lambda h: k_hbm.at[:, cols(h)], kb.at[0, x], s_kx, o) for o in range(1, X)
    ]
    for o in range(1, X):
        k_cp[o].start()

    def enter(lo, hi):
        for i in range(lo, hi):
            o = i if (i < 2 or X == 2) else X + 1 - i
            if o:
                k_cp[o].wait_recv()
            else:
                k_cp[o].wait()
            for way in (0, 1):
                ring(kb, s_k, way, 1, i).start()

    enter(0, 1)
    for o in range(1, X):
        q_cp[o].start()

    scan(True)
    for n in range(Y):
        fp[n] = jnp.exp((-SPAN * n) * rates)
    steps = lax.broadcasted_iota(jnp.int32, (SUB, W), 0).astype(jnp.float32) + 1.0
    for m in range(rates.shape[0]):
        dd[m] = wgt[m : m + 1, :] * jnp.exp(-rates[m : m + 1, :] * steps)

    enter(1, X)

    for k in range(1, Y):
        t_cp[k - 1].wait_recv()
    row_total = fp[Y - 1 - y] * tb[0]
    before = jnp.zeros_like(rates)
    for k in range(1, Y):
        part = tb[k]
        row_total = row_total + fp[Y - 1 - lax.rem(y + Y - k, Y)] * part
        before = before + jnp.where(k <= y, fp[k - 1] * part, 0.0)
    rb[0] = row_total
    r_cp = [
        remote(rb.at[0], rb.at[o], s_r, X, o, seq_id(lax.rem(x + o, X), y, c)) for o in range(1, X)
    ]
    for o in range(1, X):
        r_cp[o - 1].start()

    for o in range(X):
        if o:
            q_cp[o].wait_recv()
        else:
            q_cp[o].wait()
    qs_cp = pltpu.make_async_remote_copy(
        src_ref=qb.at[c],
        dst_ref=qb.at[c],
        send_sem=s_q.at[0],
        recv_sem=s_q.at[X],
        device_id=sib,
        device_id_type=MESH,
    )
    qs_cp.start()
    hop(kb, s_k, 2)

    for o in range(1, X):
        r_cp[o - 1].wait_recv()
    rows_before = jnp.zeros_like(rates)
    for o in range(1, X):
        fade = jnp.exp((-SPAN * Y * (o - 1)) * rates)
        rows_before = rows_before + jnp.where(o <= x, fade * rb[o], 0.0)
    part = before + fp[y] * rows_before
    e_own[...] = jnp.where(c == 0, f_one * part + total, part)
    e_cp = remote(e_own, e_sib, s_e, 1, 0, sib)
    e_cp.start()
    e_cp.wait_recv()
    carry = e_sib[...] + jnp.where(c == 0, part, f_one * part)

    in_go.wait()
    in_sg.wait()
    skip = sg_ref[...]
    for n in range(chains):
        for b in range(SUB // 8):
            r0 = n * SUB + b * 8
            acc = y0[r0 : r0 + 8, :] + skip * g[r0 : r0 + 8, :]
            for m in range(rates.shape[0]):
                acc = acc + dd[m, b * 8 : b * 8 + 8, :] * carry[m : m + 1, :]
            cv[r0 : r0 + 8, :] = go[r0 : r0 + 8, :].astype(jnp.float32) * acc
        carry = ends[n] + d_sub * carry

    squares = jnp.zeros((8, T), jnp.float32)
    for h in range(X):
        block = cv[:, h * HD : (h + 1) * HD].T
        vs[h] = block.astype(jnp.bfloat16)
        squares = squares + jnp.sum((block * block).reshape(HD // 8, 8, T), axis=0)
    in_v = pltpu.make_async_copy(vs.at[x], vb.at[0, x], s_in.at[5])
    in_v.start()
    v_cp = inject(lambda h: vs.at[h], in_v, vb, s_vx, s_v)
    sq[0] = jnp.sum(squares, axis=0, keepdims=True)
    s_cp = [
        remote(sq.at[0], sq.at[k], s_s, Z, k, {"chan": lax.rem(z + k, Z)}) for k in range(1, Z)
    ]
    for k in sorted(range(1, Z), key=lambda k: -min(k, Z - k)):
        s_cp[k - 1].start()

    to_log2 = math.log2(math.e) / math.sqrt(HD)
    delta = lax.broadcasted_iota(jnp.int32, (T, CORES * T), 0) - lax.broadcasted_iota(
        jnp.int32, (T, CORES * T), 1
    )

    def slot_of(i):
        half = (i + 1) // 2
        return jnp.where(lax.rem(i, 2) == 1, half, lax.rem(Y - half, Y))

    def weigh(j):
        from_y = lax.rem(y + Y - j, Y)
        visible = delta <= (y - from_y) * (CORES * T) - c * T
        for xp in range(X):
            n = (xp + 1) * T
            keys = kb[j, 0 : xp + 1].reshape(n, HD)
            rows = jnp.concatenate([qb[0, xp], qb[1, xp]], axis=0)
            sc = lax.dot_general(
                keys, rows, (((1,), (1,)), ((), ())), preferred_element_type=jnp.float32
            )
            edge = jnp.where(visible, sc[n - T :], NEG)
            top = jnp.max(edge, axis=0, keepdims=True)
            if xp:
                top = jnp.maximum(top, jnp.max(sc[: n - T], axis=0, keepdims=True))
            top = top * to_log2
            ex = jnp.exp2(edge * to_log2 - top)
            tot = jnp.sum(ex, axis=0, keepdims=True)
            pt[j, xp, n - T : n, :] = ex.astype(jnp.bfloat16)
            if xp:
                ex = jnp.exp2(sc[: n - T] * to_log2 - top)
                tot = tot + jnp.sum(ex, axis=0, keepdims=True)
                pt[j, xp, : n - T, :] = ex.astype(jnp.bfloat16)
            ms[j, xp : xp + 1, :] = top
            ls[j, xp : xp + 1, :] = tot

    def weigh_range(a, b):
        lax.fori_loop(a, b, lambda i, _: (weigh(slot_of(i)), 0)[1], 0)

    def mix(j, fresh=False, only=None):
        inv = [rr[j, p] for p in range(X)]
        for xp in range(X) if only is None else (only,):
            n = (xp + 1) * T
            vals = [
                (vb[j, p].astype(jnp.float32) * inv[p]).astype(jnp.bfloat16) for p in range(xp + 1)
            ]
            vals = jnp.concatenate(vals, axis=1)
            part = jnp.dot(vals, pt[j, xp, :n, :], preferred_element_type=jnp.float32)
            part = part * ms[j, xp : xp + 1, :]
            for cc in range(CORES):
                piece = part[:, cc * T : (cc + 1) * T]
                if fresh:
                    ac[cc, xp, :HD, :] = piece
                else:
                    ac[cc, xp, :HD, :] += piece

    def ry(n):
        dx, dy = lax.rem(n, X), n // X
        to = seq_id(lax.rem(x + dx, X), lax.rem(y + dy, Y), c)
        return remote(rr.at[0, x], rr.at[dy, x], s_ry, X * Y, n, to)

    def scales(j, lo=0):
        for dx in range(lo, X):
            ry(j * X + dx).wait_recv()

    qs_cp.wait_recv()
    weigh_range(0, 1)
    hop(kb, s_k, 3)
    weigh_range(1, 3)
    hop(vb, s_v, 2, 0, X // 2)
    hop(kb, s_k, 4)

    for k in range(1, Z):
        s_cp[k - 1].wait_recv()
    squares = sq[0]
    for k in range(1, Z):
        squares = squares + sq[k]
    rr[0, x] = lax.rsqrt(squares / float(W * Z) + 1e-6)
    lax.fori_loop(1, X * Y, lambda n, _: (ry(n).start(), 0)[1], 0)

    hop(vb, s_v, 2, X // 2, X)
    if D > 2:
        weigh_range(3, 5)
        hop(vb, s_v, 3)
    got(kb, s_k, D)
    weigh_range(5 if D > 2 else 3, Y)

    peak = ms[0]
    for j in range(1, Y):
        peak = jnp.maximum(peak, ms[j])
    tot = jnp.zeros_like(peak)
    for j in range(Y):
        fade = jnp.exp2(ms[j] - peak)
        tot = tot + ls[j] * fade
        ms[j] = fade
    for xp in range(X):
        for cc in range(CORES):
            ac[cc, xp, HD : HD + 1, :] = peak[xp : xp + 1, cc * T : (cc + 1) * T]
            ac[cc, xp, HD + 1 : HD + 2, :] = tot[xp : xp + 1, cc * T : (cc + 1) * T]
            ac[cc, xp, HD + 2 : HD + 8, :] = jnp.zeros((6, T), jnp.float32)

    entered(v_cp)
    scales(0, 1)
    mix(0, fresh=True)

    def mix_range(a, b):
        def body(i, _):
            j = slot_of(i)
            scales(j)
            mix(j)
            return 0

        lax.fori_loop(a, b, body, 0)

    if D > 2:
        mix_range(1, 5)
        got(vb, s_v, 3)
        mix_range(5, 7)
    else:
        mix_range(1, 3)

    def merge(xp):
        return remote(ac.at[1 - c, xp], orx.at[xp], s_m, X, xp, sib)

    got(vb, s_v, D)
    scales(D)
    for xp in reversed(range(X)):
        mix(D, only=xp)
        merge(xp).start()
    out_cp = []
    for o in sorted(range(1, X), key=lambda o: -min(o, X - o)) + [0]:
        xp = lax.rem(x + o, X)
        merge(xp).wait_recv()
        m0, m1 = ac[c, xp, HD : HD + 1, :], orx[xp, HD : HD + 1, :]
        l0, l1 = ac[c, xp, HD + 1 : HD + 2, :], orx[xp, HD + 1 : HD + 2, :]
        top = jnp.maximum(m0, m1)
        a0, a1 = jnp.exp2(m0 - top), jnp.exp2(m1 - top)
        both = (ac[c, xp, :HD, :] * a0 + orx[xp, :HD, :] * a1) / (l0 * a0 + l1 * a1)
        fs[o] = both.T.astype(jnp.bfloat16)
        if o:
            cp = remote(fs.at[o], o_ref.at[:, cols(x)], s_o, X, o, seq_id(xp, y, c))
        else:
            cp = pltpu.make_async_copy(fs.at[0], o_ref.at[:, cols(x)], s_in.at[6])
        cp.start()
        out_cp.append(cp)

    e_cp.wait_send()
    qs_cp.wait_send()
    for o in range(1, X):
        q_cp[o].wait_send()
        k_cp[o].wait_send()
        v_cp[o].wait_send()
        r_cp[o - 1].wait_send()
    for cp in t_cp + s_cp:
        cp.wait_send()
    for xp in range(X):
        merge(xp).wait_send()
    lax.fori_loop(1, X * Y, lambda n, _: (ry(n).wait_send(), 0)[1], 0)
    drain(kb, s_k)
    drain(vb, s_v)
    for cp in out_cp:
        cp.wait()


def local(X, Y, Z, go, gi, vi, pr, pw, sg, q, k):
    T, W = go.shape
    modes = pr.shape[0]
    D = Y // 2
    f32, bf16 = jnp.float32, jnp.bfloat16
    hbm = pl.BlockSpec(memory_space=pl.ANY)
    vmem = pl.BlockSpec(memory_space=pltpu.VMEM)
    dma = lambda n: pltpu.SemaphoreType.DMA((n,))
    return pl.pallas_call(
        functools.partial(kernel, X, Y, Z),
        out_shape=jax.ShapeDtypeStruct((T, W), bf16),
        in_specs=[hbm] * 8,
        out_specs=vmem,
        scratch_shapes=[
            pltpu.VMEM((modes, W), f32),
            pltpu.VMEM((modes, W), f32),
            pltpu.VMEM((1, W), f32),
            pltpu.VMEM((T, W), bf16),
            pltpu.VMEM((T, W), bf16),
            pltpu.VMEM((T, W), bf16),
            pltpu.VMEM((T, W), f32),
            pltpu.VMEM((T, W), f32),
            pltpu.VMEM((T, W), f32),
            pltpu.VMEM((modes, SUB, W), f32),
            pltpu.VMEM((Y, modes, W), f32),
            pltpu.VMEM((modes, W), f32),
            pltpu.VMEM((modes, W), f32),
            pltpu.VMEM((Y, modes, W), f32),
            pltpu.VMEM((X, modes, W), f32),
            pltpu.VMEM((Z, 1, T), f32),
            pltpu.VMEM((Y, X, 1, T), f32),
            pltpu.VMEM((X, HD, T), bf16),
            pltpu.VMEM((CORES, X, T, HD), bf16),
            pltpu.VMEM((Y, X, T, HD), bf16),
            pltpu.VMEM((Y, X, HD, T), bf16),
            pltpu.VMEM((Y, X, X * T, CORES * T), bf16),
            pltpu.VMEM((Y, X, CORES * T), f32),
            pltpu.VMEM((Y, X, CORES * T), f32),
            pltpu.VMEM((CORES, X, HD + 8, T), f32),
            pltpu.VMEM((X, HD + 8, T), f32),
            pltpu.VMEM((X, T, HD), bf16),
            dma(10),
            dma(2),
            dma(2 * Y),
            dma(2 * X),
            dma(2 * Z),
            dma(2 * X * Y),
            dma(2 * X),
            dma(2 * X),
            dma(4 * D * X),
            dma(2 * X),
            dma(4 * D * X),
            dma(2 * X),
            dma(2 * X),
        ],
        compiler_params=pltpu.CompilerParams(
            collective_id=0, has_side_effects=True, vmem_limit_bytes=67043328
        ),
    )(go, gi, vi, pr, pw, sg.reshape(1, W), q, k)


def solution(mesh, X=4, Y=8):
    Z = mesh.shape["chan"]
    rows = P("seq", "chan")
    in_specs = (rows, rows, rows, P(None, "chan"), P(None, "chan"), P("chan"), rows, rows)
    return jax.shard_map(
        functools.partial(local, X, Y, Z),
        mesh=mesh,
        in_specs=in_specs,
        out_specs=rows,
        check_vma=False,
    )
```
